32 devices in a mesh: section: 2 (over x), dp: 4 (over y, core), shard: 4 (over z).
Axes of the slice: x: 2, y: 2, z: 4, core: 2. Of those that a mesh axis runs over, the one named last changes fastest.
Arguments:
- norm_input: bfloat16 [2, 4, 512, 3584], P('section', 'dp', 'shard'), may hold values from -6 to 6
- norm_gain: float32 [2, 3584], P('section'), may hold values from 0.1 to 1.9
- branch_grad: bfloat16 [2, 4, 512, 3584], P('section', 'dp', 'shard'), may hold values from -6 to 6
- residual_grad: bfloat16 [2, 4, 512, 3584], P('section', 'dp', 'shard'), may hold values from -6 to 6
- down_weight: bfloat16 [2, 1792, 3584], P('section', 'shard'), may hold values from -0.09375 to 0.09375
Outputs:
- boundary_grad: bfloat16 [2, 4, 512, 3584], P('section', 'dp', 'shard')
- gain_grad: float32 [2, 3584], P('section')
- unit_grads: bfloat16 [2, 4, 512, 1792], P('section', 'dp', None, 'shard')
The draws below stay inside these ranges and needn't reach their ends.
All inputs are finite; a program needn't handle non-finite values.
Results may differ from the reference program's by a relative error of at most 0.0049.
Values may be sent and summed in bfloat16 or wider, within the bound.
No kernel may reach another device: no remote copies, remote signals or barrier semaphores. Data moves between devices by JAX's collectives and lax.ppermute only.
A program may use at most 128 MiB of HBM per device.

```python
import jax
import jax.numpy as jnp
from jax import lax

D = 3584
SEQ = 512
FF = 1792
BATCH = 4
SECTIONS = 2


def block_levels(key, dims, shards, smallest, top_value):
    gain, own = 1.0, jax.random.fold_in(key, 6)
    for position, shards_of in shards:
        heights = jnp.exp(jax.random.uniform(jax.random.fold_in(own, position), (shards_of,), jnp.float32, smallest / len(shards), top_value / len(shards)))
        gain = gain * jnp.repeat(heights, dims[position] // shards_of).reshape([-1 if axis == position else 1 for axis in range(len(dims))])
    return gain


def noise(rng, dims, width, most, split=(), dtype=jnp.bfloat16):
    loudness = block_levels(rng, dims, split, -0.22, 0.18) if split else 1.0
    entries = jax.random.normal(rng, dims, jnp.float32) * width * loudness
    return jnp.minimum(jnp.maximum(entries, -most), most).astype(dtype)


def setup_inputs(seed: int = 0) -> dict:
    key_list = jax.random.split(jax.random.key(seed), 6)
    norm_input = noise(key_list[0], (SECTIONS, BATCH, SEQ, D), 1.0, 6.0, ((0, 2), (1, 4), (2, 4)))
    norm_gain = jnp.clip(1.0 + 0.18 * jax.random.normal(key_list[1], (SECTIONS, D), jnp.float32), 0.1, 1.9)
    branch_grad = noise(key_list[2], (SECTIONS, BATCH, SEQ, D), 1.0, 6.0, ((0, 2), (1, 4), (2, 4)))
    residual_grad = noise(key_list[3], (SECTIONS, BATCH, SEQ, D), 1.0, 6.0, ((0, 2), (1, 4), (2, 4)))
    down_weight = noise(key_list[4], (SECTIONS, FF, D), D ** -0.5, 0.09375, ((0, 2), (1, 4)))
    return dict(norm_input=norm_input, norm_gain=norm_gain, branch_grad=branch_grad, residual_grad=residual_grad, down_weight=down_weight)


epsilon = 1e-05

def reference(norm_input, norm_gain, branch_grad, residual_grad, down_weight):
    values = norm_input.astype(jnp.float32)
    inverse = lax.rsqrt(lax.optimization_barrier(jnp.mean(values * values, axis=-1, keepdims=True)) + epsilon)
    normed = values * inverse
    upstream = branch_grad.astype(jnp.float32)
    scaled = upstream * norm_gain[:, None, None, :]
    project = lax.optimization_barrier(jnp.mean(scaled * normed, axis=-1, keepdims=True))
    boundary = (residual_grad.astype(jnp.float32) + inverse * (scaled - normed * project)).astype(jnp.bfloat16)
    gain_grad = lax.optimization_barrier(jnp.sum(upstream * normed, axis=(1, 2))) / SEQ
    arrived = jnp.flip(boundary, axis=0).astype(jnp.float32)
    unit_grads = jnp.einsum('gbsd,ghd->gbsh', arrived, down_weight.astype(jnp.float32), precision=lax.Precision.HIGHEST).astype(jnp.bfloat16)
    return (boundary, gain_grad, unit_grads)
```

```python
import functools
import math

import jax
import jax.numpy as jnp
from jax import lax
from jax.experimental import pallas as pl
from jax.experimental.pallas import tpu as pltpu
from jax.sharding import PartitionSpec as P

epsilon = 1e-05


def norm_kernel(width, group, x_ref, gain_ref, up_ref, res_ref, out_ref, lo_ref, hi_ref, sum_ref, part_ref):
    rows, dim = x_ref.shape
    half = lo_ref.shape[1]
    f32 = jnp.float32

    @pl.when(pl.program_id(0) == 0)
    def _():
        part_ref[...] = jnp.zeros_like(part_ref)

    @pl.loop(0, rows // group)
    def _(step):
        here = pl.ds(pl.multiple_of(step * group, group), group)
        squares = jnp.zeros((group, 128), f32)
        cross = jnp.zeros((group, 128), f32)
        for at in range(0, dim, width):
            cols = slice(at, at + width)
            v = x_ref[here, cols].astype(f32)
            s = up_ref[here, cols].astype(f32) * gain_ref[:, cols]
            vv, sv = v * v, s * v
            for lane in range(0, width, 128):
                squares += vv[:, lane : lane + 128]
                cross += sv[:, lane : lane + 128]
        inverse = lax.rsqrt(jnp.sum(squares, axis=-1, keepdims=True) / dim + epsilon)
        project = inverse * (jnp.sum(cross, axis=-1, keepdims=True) / dim)
        for at in range(0, dim, width):
            cols = slice(at, at + width)
            u = up_ref[here, cols].astype(f32)
            normed = x_ref[here, cols].astype(f32) * inverse
            moved = inverse * (u * gain_ref[:, cols] - normed * project)
            b = (res_ref[here, cols].astype(f32) + moved).astype(jnp.bfloat16)
            out_ref[here, cols] = b
            if at < half:
                lo_ref[here, cols] = b
            else:
                hi_ref[here, at - half : at - half + width] = b
            terms = u * normed
            part_ref[:, cols] += functools.reduce(jnp.add, [terms[at : at + 8] for at in range(0, group, 8)])

    @pl.when(pl.program_id(0) == pl.num_programs(0) - 1)
    def _():
        sum_ref[...] = jnp.sum(part_ref[...], axis=0, keepdims=True)


def norm_backward(x, gain, up, res):
    rows, dim = x.shape
    half = dim // 2
    block = math.gcd(rows, 64)
    span = lambda cols: pl.BlockSpec((block, cols), lambda i: (i, 0))
    row = pl.BlockSpec((1, dim), lambda i: (0, 0))
    shape = jax.ShapeDtypeStruct
    return pl.pallas_call(
        functools.partial(norm_kernel, math.gcd(half, 256), math.gcd(block, 32)),
        grid=(rows // block,),
        in_specs=[span(dim), row, span(dim), span(dim)],
        out_specs=[span(dim), span(half), span(half), row],
        out_shape=[
            shape((rows, dim), jnp.bfloat16),
            shape((rows, half), jnp.bfloat16),
            shape((rows, half), jnp.bfloat16),
            shape((1, dim), jnp.float32),
        ],
        scratch_shapes=[pltpu.VMEM((8, dim), jnp.float32)],
        cost_estimate=pl.CostEstimate(flops=12 * rows * dim, bytes_accessed=10 * rows * dim, transcendentals=rows),
        name="norm_backward",
    )(x, gain, up, res)


def dot(w, t):
    return lax.dot_general(w, t, (((1,), (1,)), ((), ())), preferred_element_type=jnp.float32)


def swap(axis, distance):
    count = lax.axis_size(axis)
    return [(at, at ^ distance) for at in range(count)]


def send(block, axis, route):
    return lax.ppermute(block, axis, route)


def relay(norm_input, norm_gain, branch_grad, residual_grad, down_weight):
    weight = down_weight[0]
    hidden, dim = weight.shape
    copies = lax.axis_size("dp")
    me_dp, me = lax.axis_index("dp"), lax.axis_index("shard")
    last = lax.axis_size("shard") - 1
    flip = lambda at: last - at
    both = lambda route: route + [(flip(a), flip(b)) for a, b in route]
    inward, across, outward = both([(0, 1)]), both([(1, 2)]), both([(1, 0)])
    count = last + 1
    cross = lambda route: [((1 - g) * count + a, g * count + b) for g in (0, 1) for a, b in route]
    other = ("section", "shard")

    part = hidden // copies
    piece = lax.dynamic_slice_in_dim(weight, me_dp * part, part, axis=0)
    pieces = [send(piece, "shard", inward)]
    boundary, lo, hi, gain = norm_backward(norm_input[0, 0], norm_gain, branch_grad[0, 0], residual_grad[0, 0])

    ends = cross(both([(0, 0)]))
    outer_lo = send(lo, other, ends)
    far = send(boundary, other, cross(across))
    outer_hi = send(hi, other, ends)

    distance = 1
    while distance < copies:
        gain = gain + send(gain, "dp", swap("dp", distance))
        distance *= 2
    edge_lo = send(outer_lo, "shard", inward)
    summed = [send(gain, "shard", inward), send(gain, "shard", both([(0, 2)])), send(gain, "shard", across)]
    gain = functools.reduce(jnp.add, summed, gain)
    edge_hi = send(outer_hi, "shard", inward)

    distance = copies // 2
    orders = [0]
    while distance:
        pieces = pieces + [send(p, "dp", swap("dp", distance)) for p in pieces]
        orders = orders + [at ^ distance for at in orders]
        distance //= 2
    edge_weight = jnp.concatenate([p for _, p in sorted(zip(orders, pieces), key=lambda t: t[0])])

    gain_out = send(gain, "shard", outward)
    near = send(boundary, other, cross(both([(1, 1)])))
    tail_lo = send(edge_lo, "shard", across)
    tail_hi = send(edge_hi, "shard", across)

    rows, half = lo.shape
    bf16 = jnp.bfloat16
    low, high = slice(0, half), slice(half, dim)
    own, edge = {}, {}
    own["far"] = dot(weight, far).astype(bf16)
    own_half = dot(weight[:, low], edge_lo)
    edge["far"] = dot(edge_weight, far).astype(bf16)
    edge["edge"] = (dot(edge_weight[:, low], edge_lo) + dot(edge_weight[:, high], edge_hi)).astype(bf16)
    early = jnp.concatenate([edge["far"], edge["edge"]], axis=1)
    one = send(early, "shard", outward)
    near, edge_hi, early = lax.optimization_barrier((near, edge_hi, early))
    edge["near"] = dot(edge_weight, near).astype(bf16)
    two = send(edge["near"], "shard", outward)
    begun = dot(edge_weight[:, low], tail_lo)
    own["edge"] = (own_half + dot(weight[:, high], edge_hi)).astype(bf16)
    tail_hi, own["far"], own["edge"], begun = lax.optimization_barrier((tail_hi, own["far"], own["edge"], begun))
    edge["tail"] = (begun + dot(edge_weight[:, high], tail_hi)).astype(bf16)
    three = send(edge["tail"], "shard", outward)
    tail_lo, tail_hi, near, _ = lax.optimization_barrier((tail_lo, tail_hi, near, edge["tail"]))
    own["near"] = dot(weight, near).astype(bf16)
    own["tail"] = (dot(weight[:, low], tail_lo) + dot(weight[:, high], tail_hi)).astype(bf16)
    one, two, own["near"], own["tail"] = lax.optimization_barrier((one, two, own["near"], own["tail"]))
    inner = (me != 0) & (me != last)
    gain_grad = jnp.where(inner, gain, gain_out) / (rows * count)

    def restore(block):
        block = block.reshape(copies, part, rows)
        distance = 1
        while distance < copies:
            order = [at ^ distance for at in range(copies)]
            moved = jnp.stack([block[at] for at in order])
            block = jnp.where((me_dp & distance) != 0, moved, block)
            distance *= 2
        return block.reshape(hidden, rows)

    got = {"far": one[:, :rows], "edge": one[:, rows:], "near": two}
    result = {name: jnp.where(inner, own[name], restore(got[name])) for name in got}
    names = tuple(result)
    ready = lax.optimization_barrier((three, own["tail"], gain_grad) + tuple(result[name] for name in names))
    three, own["tail"], gain_grad = ready[:3]
    result = dict(zip(names, ready[3:]))
    result["tail"] = jnp.where(inner, own["tail"], restore(three))
    up = jnp.concatenate([result[name] for name in ("edge", "near", "far", "tail")], axis=1)
    down = jnp.concatenate([result[name] for name in ("tail", "far", "near", "edge")], axis=1)
    fresh = jnp.where(me < count // 2, up, down).T
    return (boundary[None, None], gain_grad, fresh[None, None])


def gather(norm_input, norm_gain, branch_grad, residual_grad, down_weight):
    boundary, _, _, gain = norm_backward(norm_input[0, 0], norm_gain, branch_grad[0, 0], residual_grad[0, 0])
    arrived = lax.ppermute(boundary, "section", swap("section", 1))
    fresh = jnp.einsum(
        "nd,hd->nh",
        lax.all_gather(arrived, "shard", axis=0, tiled=True),
        down_weight[0],
        preferred_element_type=jnp.float32,
    ).astype(jnp.bfloat16)
    gain_grad = lax.psum(gain, ("dp", "shard")) / fresh.shape[0]
    return (boundary[None, None], gain_grad, fresh[None, None])


def solution(mesh):
    in_specs = (
        P("section", "dp", "shard", None),
        P("section", None),
        P("section", "dp", "shard", None),
        P("section", "dp", "shard", None),
        P("section", "shard", None),
    )
    out_specs = (
        P("section", "dp", "shard", None),
        P("section", None),
        P("section", "dp", None, "shard"),
    )
    line = mesh.shape["shard"] == 4 and mesh.shape["section"] == 2
    mapped = functools.partial(jax.shard_map, mesh=mesh, in_specs=in_specs, out_specs=out_specs, check_vma=False)
    if not line:
        return mapped(gather)
    return mapped(relay)
```

```python
import functools
import math

import jax
import jax.numpy as jnp
from jax import lax
from jax.experimental import pallas as pl
from jax.experimental.pallas import tpu as pltpu
from jax.sharding import PartitionSpec as P

epsilon = 1e-05

CUTS = 1
CHUNKS = 3


def spans_of(dim, count):
    lanes = dim // 128
    edges = [128 * (lanes * at // count) for at in range(count)] + [dim]
    return [slice(a, b) for a, b in zip(edges, edges[1:])]


def norm_kernel(width, group, spans, x_ref, gain_ref, up_ref, res_ref, out_ref, *refs):
    chunk_refs, sum_ref, part_ref = refs[: len(spans)], refs[-2], refs[-1]
    rows, dim = x_ref.shape
    f32 = jnp.float32

    @pl.when(pl.program_id(0) == 0)
    def _():
        part_ref[...] = jnp.zeros_like(part_ref)

    @pl.loop(0, rows // group)
    def _(step):
        here = pl.ds(pl.multiple_of(step * group, group), group)
        squares = jnp.zeros((group, 128), f32)
        cross = jnp.zeros((group, 128), f32)
        for at in range(0, dim, width):
            cols = slice(at, at + width)
            v = x_ref[here, cols].astype(f32)
            s = up_ref[here, cols].astype(f32) * gain_ref[:, cols]
            vv, sv = v * v, s * v
            for lane in range(0, width, 128):
                squares += vv[:, lane : lane + 128]
                cross += sv[:, lane : lane + 128]
        inverse = lax.rsqrt(jnp.sum(squares, axis=-1, keepdims=True) / dim + epsilon)
        project = inverse * (jnp.sum(cross, axis=-1, keepdims=True) / dim)
        for at in range(0, dim, width):
            cols = slice(at, at + width)
            u = up_ref[here, cols].astype(f32)
            normed = x_ref[here, cols].astype(f32) * inverse
            moved = inverse * (u * gain_ref[:, cols] - normed * project)
            b = (res_ref[here, cols].astype(f32) + moved).astype(jnp.bfloat16)
            out_ref[here, cols] = b
            for span, ref in zip(spans, chunk_refs):
                if span.start <= at < span.stop:
                    ref[here, at - span.start : at - span.start + width] = b
            terms = u * normed
            part_ref[:, cols] += functools.reduce(jnp.add, [terms[at : at + 8] for at in range(0, group, 8)])

    @pl.when(pl.program_id(0) == pl.num_programs(0) - 1)
    def _():
        sum_ref[...] = jnp.sum(part_ref[...], axis=0, keepdims=True)


def norm_backward(x, gain, up, res, spans=()):
    rows, dim = x.shape
    block = math.gcd(rows, 64)
    width = functools.reduce(math.gcd, [s.start for s in spans], math.gcd(dim, 256))
    tile = lambda cols: pl.BlockSpec((block, cols), lambda i: (i, 0))
    row = pl.BlockSpec((1, dim), lambda i: (0, 0))
    shape = jax.ShapeDtypeStruct
    widths = [dim] + [s.stop - s.start for s in spans]
    results = pl.pallas_call(
        functools.partial(norm_kernel, width, math.gcd(block, 32), spans),
        grid=(rows // block,),
        in_specs=[tile(dim), row, tile(dim), tile(dim)],
        out_specs=[tile(w) for w in widths] + [row],
        out_shape=[shape((rows, w), jnp.bfloat16) for w in widths] + [shape((1, dim), jnp.float32)],
        scratch_shapes=[pltpu.VMEM((8, dim), jnp.float32)],
        cost_estimate=pl.CostEstimate(flops=12 * rows * dim, bytes_accessed=10 * rows * dim, transcendentals=rows),
        compiler_params=pltpu.CompilerParams(vmem_limit_bytes=61 * 2**20),
        name="norm_backward",
    )(x, gain, up, res)
    return results[0], results[1:-1], results[-1]


def dot(w, t):
    return lax.dot_general(w, t, (((1,), (1,)), ((), ())), preferred_element_type=jnp.float32)


def swap(axis, distance):
    count = lax.axis_size(axis)
    return [(at, at ^ distance) for at in range(count)]


def relay(norm_input, norm_gain, branch_grad, residual_grad, down_weight):
    weight = down_weight[0]
    hidden, dim = weight.shape
    copies = lax.axis_size("dp")
    me_dp, me = lax.axis_index("dp"), lax.axis_index("shard")
    last = lax.axis_size("shard") - 1
    flip = lambda at: last - at
    both = lambda route: route + [(flip(a), flip(b)) for a, b in route]
    inner, lower = (me != 0) & (me != last), me <= last // 2
    flags = [inner, lower] + [(me_dp & 1 << bit) != 0 for bit in range(copies.bit_length() - 1)]
    norm_input, (inner, lower, *crossed) = lax.optimization_barrier((norm_input, flags))
    inward, across, outward = both([(0, 1)]), both([(1, 2)]), both([(1, 0)])
    count = last + 1
    cross = lambda route: [((1 - g) * count + a, g * count + b) for g in (0, 1) for a, b in route]
    other = ("section", "shard")

    part = hidden // copies
    slab = part // CUTS
    spans = spans_of(dim, CHUNKS)
    bf16 = jnp.bfloat16

    pieces = []
    for cut in range(CUTS):
        piece = lax.dynamic_slice_in_dim(weight, me_dp * part + cut * slab, slab, axis=0)
        pieces.append((0, cut, lax.ppermute(piece, "shard", inward)))
    boundary, chunks, gain = norm_backward(
        norm_input[0, 0], norm_gain, branch_grad[0, 0], residual_grad[0, 0], spans
    )
    rows = boundary.shape[0]

    ends = cross(both([(0, 0)]))
    far = lax.ppermute(boundary, other, cross(across))
    near = lax.ppermute(boundary, other, cross(both([(1, 1)])))
    outer = [lax.ppermute(chunk, other, ends) for chunk in chunks]
    rim = [lax.ppermute(chunk, "shard", inward) for chunk in outer]
    tail = [lax.ppermute(chunk, "shard", across) for chunk in rim]

    distance = 1
    while distance < copies:
        gain = gain + lax.ppermute(gain, "dp", swap("dp", distance))
        distance *= 2
    for route in (inward, across):
        moved = lax.ppermute(gain, "shard", route)
        gain = gain + moved
    gain_out = lax.ppermute(gain, "shard", outward)

    distance = copies // 2
    while distance:
        pieces += [
            (at ^ distance, cut, lax.ppermute(block, "dp", swap("dp", distance)))
            for at, cut, block in list(pieces)
        ]
        distance //= 2
    edge_weight = jnp.concatenate([block for _, _, block in sorted(pieces, key=lambda t: t[:2])])

    def whole(w, t):
        return [dot(w, t)]

    def parts(w, blocks):
        return [dot(w[:, s], block) for s, block in zip(spans, blocks)]

    def total(terms):
        return functools.reduce(jnp.add, terms).astype(bf16)

    own, edge = {}, {}
    edge["far"] = total(whole(edge_weight, far))
    local = total(parts(weight, outer))
    one = lax.ppermute(edge["far"], "shard", outward)
    near, edge["far"] = lax.optimization_barrier((near, edge["far"]))
    edge["near"] = dot(edge_weight, near).astype(bf16)
    two = lax.ppermute(edge["near"], "shard", outward)
    begun = parts(edge_weight, tail[:-1])
    tail[-1], begun = lax.optimization_barrier((tail[-1], begun))
    edge["tail"] = total(begun + [dot(edge_weight[:, spans[-1]], tail[-1])])
    three = lax.ppermute(edge["tail"], "shard", outward)
    far, rim, near, tail, _ = lax.optimization_barrier((far, rim, near, tail, edge["tail"]))
    own["far"] = total(whole(weight, far))
    own["edge"] = total(parts(weight, rim))
    own["near"] = dot(weight, near).astype(bf16)
    own["tail"] = total(parts(weight, tail))
    one, two, own, local = lax.optimization_barrier((one, two, own, local))
    gain_grad = jnp.where(inner, gain, gain_out) / (rows * count)

    def restore(block):
        block = block.reshape(copies, part, rows)
        for bit, flip in enumerate(crossed):
            moved = jnp.stack([block[at ^ 1 << bit] for at in range(copies)])
            block = jnp.where(flip, moved, block)
        return block.reshape(hidden, rows)

    got = {"far": restore(one), "near": restore(two), "edge": local}
    result = {name: jnp.where(inner, own[name], got[name]) for name in got}
    names = tuple(result)
    ready = lax.optimization_barrier((three, own["tail"], gain_grad) + tuple(result[name] for name in names))
    three, own["tail"], gain_grad = ready[:3]
    result = dict(zip(names, ready[3:]))
    result["tail"] = jnp.where(inner, own["tail"], restore(three))
    up = jnp.concatenate([result[name] for name in ("edge", "near", "far", "tail")], axis=1)
    down = jnp.concatenate([result[name] for name in ("tail", "far", "near", "edge")], axis=1)
    fresh = jnp.where(lower, up, down).T
    return (boundary[None, None], gain_grad, fresh[None, None])


def gather(norm_input, norm_gain, branch_grad, residual_grad, down_weight):
    boundary, _, gain = norm_backward(norm_input[0, 0], norm_gain, branch_grad[0, 0], residual_grad[0, 0])
    arrived = lax.ppermute(boundary, "section", swap("section", 1))
    fresh = jnp.einsum(
        "nd,hd->nh",
        lax.all_gather(arrived, "shard", axis=0, tiled=True),
        down_weight[0],
        preferred_element_type=jnp.float32,
    ).astype(jnp.bfloat16)
    gain_grad = lax.psum(gain, ("dp", "shard")) / fresh.shape[0]
    return (boundary[None, None], gain_grad, fresh[None, None])


def solution(mesh):
    in_specs = (
        P("section", "dp", "shard", None),
        P("section", None),
        P("section", "dp", "shard", None),
        P("section", "dp", "shard", None),
        P("section", "shard", None),
    )
    out_specs = (
        P("section", "dp", "shard", None),
        P("section", None),
        P("section", "dp", None, "shard"),
    )
    line = mesh.shape["shard"] == 4 and mesh.shape["section"] == 2
    mapped = functools.partial(jax.shard_map, mesh=mesh, in_specs=in_specs, out_specs=out_specs, check_vma=False)
    if not line:
        return mapped(gather)
    return mapped(relay)
```

```python
import functools
import math

import jax
import jax.numpy as jnp
from jax import lax
from jax.experimental import pallas as pl
from jax.experimental.pallas import tpu as pltpu
from jax.sharding import PartitionSpec as P

epsilon = 1e-05

CUTS = 1
CHUNKS = 3


def spans_of(dim, count):
    lanes = dim // 128
    edges = [128 * -(-lanes * at // count) for at in range(count)] + [dim]
    return [slice(a, b) for a, b in zip(edges, edges[1:])]


def norm_kernel(width, group, spans, x_ref, gain_ref, up_ref, res_ref, out_ref, *refs):
    chunk_refs, sum_ref, part_ref = refs[: len(spans)], refs[-2], refs[-1]
    rows, dim = x_ref.shape
    f32 = jnp.float32

    @pl.when(pl.program_id(0) == 0)
    def _():
        part_ref[...] = jnp.zeros_like(part_ref)

    @pl.loop(0, rows // group)
    def _(step):
        here = pl.ds(pl.multiple_of(step * group, group), group)
        squares = jnp.zeros((group, 128), f32)
        cross = jnp.zeros((group, 128), f32)
        for at in range(0, dim, width):
            cols = slice(at, at + width)
            v = x_ref[here, cols].astype(f32)
            s = up_ref[here, cols].astype(f32) * gain_ref[:, cols]
            vv, sv = v * v, s * v
            for lane in range(0, width, 128):
                squares += vv[:, lane : lane + 128]
                cross += sv[:, lane : lane + 128]
        inverse = lax.rsqrt(jnp.sum(squares, axis=-1, keepdims=True) / dim + epsilon)
        project = inverse * (jnp.sum(cross, axis=-1, keepdims=True) / dim)
        for at in range(0, dim, width):
            cols = slice(at, at + width)
            u = up_ref[here, cols].astype(f32)
            normed = x_ref[here, cols].astype(f32) * inverse
            moved = inverse * (u * gain_ref[:, cols] - normed * project)
            b = (res_ref[here, cols].astype(f32) + moved).astype(jnp.bfloat16)
            out_ref[here, cols] = b
            for span, ref in zip(spans, chunk_refs):
                if span.start <= at < span.stop:
                    ref[here, at - span.start : at - span.start + width] = b
            terms = u * normed
            part_ref[:, cols] += functools.reduce(jnp.add, [terms[at : at + 8] for at in range(0, group, 8)])

    @pl.when(pl.program_id(0) == pl.num_programs(0) - 1)
    def _():
        sum_ref[...] = jnp.sum(part_ref[...], axis=0, keepdims=True)


def norm_backward(x, gain, up, res, spans=()):
    rows, dim = x.shape
    block = math.gcd(rows, 64)
    width = functools.reduce(math.gcd, [s.start for s in spans], math.gcd(dim, 256))
    tile = lambda cols: pl.BlockSpec((block, cols), lambda i: (i, 0))
    row = pl.BlockSpec((1, dim), lambda i: (0, 0))
    shape = jax.ShapeDtypeStruct
    widths = [dim] + [s.stop - s.start for s in spans]
    results = pl.pallas_call(
        functools.partial(norm_kernel, width, math.gcd(block, 32), spans),
        grid=(rows // block,),
        in_specs=[tile(dim), row, tile(dim), tile(dim)],
        out_specs=[tile(w) for w in widths] + [row],
        out_shape=[shape((rows, w), jnp.bfloat16) for w in widths] + [shape((1, dim), jnp.float32)],
        scratch_shapes=[pltpu.VMEM((8, dim), jnp.float32)],
        cost_estimate=pl.CostEstimate(flops=12 * rows * dim, bytes_accessed=10 * rows * dim, transcendentals=rows),
        compiler_params=pltpu.CompilerParams(vmem_limit_bytes=61 * 2**20),
        name="norm_backward",
    )(x, gain, up, res)
    return results[0], results[1:-1], results[-1]


def dot(w, t):
    return lax.dot_general(w, t, (((1,), (1,)), ((), ())), preferred_element_type=jnp.float32)


def swap(axis, distance):
    count = lax.axis_size(axis)
    return [(at, at ^ distance) for at in range(count)]


def relay(norm_input, norm_gain, branch_grad, residual_grad, down_weight):
    weight = down_weight[0]
    hidden, dim = weight.shape
    copies = lax.axis_size("dp")
    me_dp, me = lax.axis_index("dp"), lax.axis_index("shard")
    last = lax.axis_size("shard") - 1
    flip = lambda at: last - at
    both = lambda route: route + [(flip(a), flip(b)) for a, b in route]
    inner, lower = (me != 0) & (me != last), me <= last // 2
    flags = [inner, lower] + [(me_dp & 1 << bit) != 0 for bit in range(copies.bit_length() - 1)]
    norm_input, (inner, lower, *crossed) = lax.optimization_barrier((norm_input, flags))
    inward, across, outward = both([(0, 1)]), both([(1, 2)]), both([(1, 0)])
    count = last + 1
    cross = lambda route: [((1 - g) * count + a, g * count + b) for g in (0, 1) for a, b in route]
    other = ("section", "shard")

    part = hidden // copies
    slab = part // CUTS
    spans = spans_of(dim, CHUNKS)
    bf16 = jnp.bfloat16

    pieces = []
    for cut in range(CUTS):
        piece = lax.dynamic_slice_in_dim(weight, me_dp * part + cut * slab, slab, axis=0)
        pieces.append((0, cut, lax.ppermute(piece, "shard", inward)))
    boundary, chunks, gain = norm_backward(
        norm_input[0, 0], norm_gain, branch_grad[0, 0], residual_grad[0, 0], spans
    )
    rows = boundary.shape[0]

    ends = cross(both([(0, 0)]))
    far = lax.ppermute(boundary, other, cross(across))
    near = lax.ppermute(boundary, other, cross(both([(1, 1)])))
    outer = [lax.ppermute(chunk, other, ends) for chunk in chunks]
    rim = [lax.ppermute(chunk, "shard", inward) for chunk in outer]
    tail = [lax.ppermute(chunk, "shard", across) for chunk in rim]

    distance = 1
    while distance < copies:
        gain = gain + lax.ppermute(gain, "dp", swap("dp", distance))
        distance *= 2
    routes = (inward, both([(0, 2)]), across)
    summed = [lax.ppermute(gain, "shard", route) for route in routes]
    gain = functools.reduce(jnp.add, summed, gain)
    gain_out = lax.ppermute(gain, "shard", outward)

    distance = copies // 2
    while distance:
        pieces += [
            (at ^ distance, cut, lax.ppermute(block, "dp", swap("dp", distance)))
            for at, cut, block in list(pieces)
        ]
        distance //= 2
    edge_weight = jnp.concatenate([block for _, _, block in sorted(pieces, key=lambda t: t[:2])])

    def whole(w, t):
        return [dot(w, t)]

    def parts(w, blocks):
        return [dot(w[:, s], block) for s, block in zip(spans, blocks)]

    def total(terms):
        return functools.reduce(jnp.add, terms).astype(bf16)

    own, edge = {}, {}
    edge["far"] = total(whole(edge_weight, far))
    local = total(parts(weight, outer))
    one = lax.ppermute(edge["far"], "shard", outward)
    tail[:-1], edge["far"] = lax.optimization_barrier((tail[:-1], edge["far"]))
    begun = parts(edge_weight, tail[:-1])
    near, begun = lax.optimization_barrier((near, begun))
    edge["near"] = dot(edge_weight, near).astype(bf16)
    two = lax.ppermute(edge["near"], "shard", outward)
    tail[-1], edge["near"] = lax.optimization_barrier((tail[-1], edge["near"]))
    edge["tail"] = total(begun + [dot(edge_weight[:, spans[-1]], tail[-1])])
    three = lax.ppermute(edge["tail"], "shard", outward)
    far, rim, near, tail, _ = lax.optimization_barrier((far, rim, near, tail, edge["tail"]))
    own["far"] = total(whole(weight, far))
    own["edge"] = total(parts(weight, rim))
    own["near"] = dot(weight, near).astype(bf16)
    own["tail"] = total(parts(weight, tail))
    one, two, own, local = lax.optimization_barrier((one, two, own, local))
    gain_grad = jnp.where(inner, gain, gain_out) / (rows * count)

    def restore(block):
        block = block.reshape(copies, part, rows)
        for bit, flip in enumerate(crossed):
            moved = jnp.stack([block[at ^ 1 << bit] for at in range(copies)])
            block = jnp.where(flip, moved, block)
        return block.reshape(hidden, rows)

    got = {"far": restore(one), "near": restore(two), "edge": local}
    result = {name: jnp.where(inner, own[name], got[name]) for name in got}
    names = tuple(result)
    ready = lax.optimization_barrier((three, own["tail"], gain_grad) + tuple(result[name] for name in names))
    three, own["tail"], gain_grad = ready[:3]
    result = dict(zip(names, ready[3:]))
    result["tail"] = jnp.where(inner, own["tail"], restore(three))
    up = jnp.concatenate([result[name] for name in ("edge", "near", "far", "tail")], axis=1)
    down = jnp.concatenate([result[name] for name in ("tail", "far", "near", "edge")], axis=1)
    fresh = jnp.where(lower, up, down).T
    return (boundary[None, None], gain_grad, fresh[None, None])


def gather(norm_input, norm_gain, branch_grad, residual_grad, down_weight):
    boundary, _, gain = norm_backward(norm_input[0, 0], norm_gain, branch_grad[0, 0], residual_grad[0, 0])
    arrived = lax.ppermute(boundary, "section", swap("section", 1))
    fresh = jnp.einsum(
        "nd,hd->nh",
        lax.all_gather(arrived, "shard", axis=0, tiled=True),
        down_weight[0],
        preferred_element_type=jnp.float32,
    ).astype(jnp.bfloat16)
    gain_grad = lax.psum(gain, ("dp", "shard")) / fresh.shape[0]
    return (boundary[None, None], gain_grad, fresh[None, None])


def solution(mesh):
    in_specs = (
        P("section", "dp", "shard", None),
        P("section", None),
        P("section", "dp", "shard", None),
        P("section", "dp", "shard", None),
        P("section", "shard", None),
    )
    out_specs = (
        P("section", "dp", "shard", None),
        P("section", None),
        P("section", "dp", None, "shard"),
    )
    line = mesh.shape["shard"] == 4 and mesh.shape["section"] == 2
    mapped = functools.partial(jax.shard_map, mesh=mesh, in_specs=in_specs, out_specs=out_specs, check_vma=False)
    if not line:
        return mapped(gather)
    return mapped(relay)
```
